256 devices in a mesh: expert: 64 (over z, y, core), dp: 4 (over x).
Axes of the slice: x: 4, y: 4, z: 8, core: 2. Of those that a mesh axis runs over, the one named last changes fastest.
Arguments:
- tokens: bfloat16 [32768, 2048], P(('dp', 'expert')), parts along dimension 0, may hold values from -6 to 6
- expert_ids: int32 [32768, 8], P(('dp', 'expert')), parts along dimension 0, may hold values from 0 to 63, all different within a row; in each aligned block of 128 rows (0 to 127, 128 to 255, ...) at most 18 rows name the same one
- route_weight: float32 [32768, 8], P(('dp', 'expert')), parts along dimension 0, may hold values from 0.05 to 1
- w_gate: bfloat16 [64, 2, 2048, 384], P('expert'), may hold values from -0.125 to 0.125
- w_up: bfloat16 [64, 2, 2048, 384], P('expert'), may hold values from -0.125 to 0.125
- w_down: bfloat16 [64, 2, 384, 2048], P('expert'), may hold values from -0.21875 to 0.21875
Outputs:
- mixed: bfloat16 [32768, 2048], P(('dp', 'expert')), parts along dimension 0
The draws below stay inside these ranges and needn't reach their ends.
There are 4 independent parts, one for each index of `dp`. The reference program is written for one: setup_inputs(seed, part) draws one part's arguments, and reference() takes and returns one part's arrays. A program takes and returns all parts, laid end to end along the dimension named above; an argument that names none is the same for every part. Nothing has to cross between parts.
Inputs may be any that keep to these rules, and one draw needn't show every extreme that they name: `expert_ids`: each row names 8 different experts. In the rows of one device (aligned blocks of 128 rows) no expert is named by more than 18 rows, a bound that some block reaches.
All inputs are finite; a program needn't handle non-finite values.
Results may differ from the reference program's by a relative error of at most 0.0071.
Values may be sent and summed in bfloat16 or wider, within the bound.
No kernel may reach another device: no remote copies, remote signals or barrier semaphores. Data moves between devices by JAX's collectives and lax.ppermute only.
A program may use at most 128 MiB of HBM per device.

```python
import math
import jax
import jax.numpy as jnp
import numpy as np
from jax import lax

D = 2048
HID = 768
TOPK = 8
TOK_DEV = 128
HALF = 384
EXPERTS = 64
CAP = 18
TOKENS = 8192
N_EXPERT = 64


def steps_of(key, shape, pieces, low, top_value):
    factor_of = 1.0
    for dim, parts in pieces:
        steps = jax.random.uniform(jax.random.fold_in(jax.random.fold_in(key, 6), dim), (parts,), jnp.float32, low / len(pieces), top_value / len(pieces))
        factor_of = factor_of * jnp.repeat(jnp.exp(steps), shape[dim] // parts).reshape((-1,) + (1,) * (len(shape) - 1 - dim))
    return factor_of


def shared_out(rng, own, number, rows, amount, top, most, skew):
    sequence = jax.random.permutation(rng, amount)
    packed, common = load_shares(amount, rows * top, most, skew, True), load_shares(amount, rows * top, most, skew, False)
    places = jnp.arange(amount)

    def named(lengths, turn):
        used = int((lengths > 0).sum())
        fixed = max(1, used // 4)
        shifted = fixed + (places - fixed + turn * (used - fixed)) % max(1, amount - fixed)
        return jnp.zeros((amount,), jnp.int32).at[sequence[jnp.where(places < fixed, places, shifted)]].set(jnp.asarray(lengths, jnp.int32))

    lengths = jnp.where(number % 4 == 0, named(packed, number // 4), named(common, number - number // 4 - 1))
    mixed = jax.random.permutation(jax.random.fold_in(own, 3), amount)
    donor, taker = mixed[0:amount // 2 * 2:2], mixed[1:amount // 2 * 2:2]
    slack = jnp.minimum(lengths[donor] - 1, most - lengths[taker]) // 2
    slack = jnp.where((donor == sequence[0]) | (taker == sequence[0]) | (lengths[taker] == 0), 0, jnp.maximum(slack, 0))
    shifted = jax.random.randint(jax.random.fold_in(own, 4), (amount // 2,), 0, 1 << 20) % (slack + 1)
    lengths = lengths.at[donor].add(-shifted).at[taker].add(shifted)
    items = jnp.searchsorted(jnp.cumsum(lengths), jnp.arange(rows * top), side="right").astype(jnp.int32)
    listing = items.reshape(top, rows).T
    listing = listing[jax.random.permutation(jax.random.fold_in(own, 1), rows)]
    turn = jax.random.randint(jax.random.fold_in(own, 2), (rows, 1), 0, top)
    return jnp.take_along_axis(listing, (jnp.arange(top)[None, :] + turn) % top, axis=1)


def load_shares(amount, total, bound, lean, full):
    weights = [(1 << 20) // math.isqrt(grade ** lean) + 1 for grade in range(1, amount + 1)]
    largest = bound if full else min(bound, max(-(-total // amount), total * weights[0] // sum(weights)))
    least = 1 if total - largest >= amount - 1 else 0
    given, surplus = [largest] + [least] * (amount - 1), total - largest - least * (amount - 1)
    while surplus > 0:
        candidates = [i for i in range(1, amount) if given[i] < largest] or [i for i in range(1, amount) if given[i] < bound]
        whole, left = sum([weights[i] for i in candidates]), surplus
        for i in candidates:
            extra = min(bound - given[i], max(1, left * weights[i] // whole), surplus)
            given[i] = given[i] + extra
            surplus = surplus - extra
    return np.array(given)


def scatter_about(key, dims, width, reach, split=(), held_as=jnp.bfloat16):
    drawn = width * jax.random.normal(key, dims, jnp.float32)
    if split:
        drawn = drawn * steps_of(key, dims, split, -0.22, 0.18)
    return jnp.clip(drawn, -reach, reach).astype(held_as)


def setup_inputs(seed: int = 0, part: int = 0) -> dict:
    arg_keys = jax.random.split(jax.random.key(seed), 7)
    part_keys = jax.random.split(jax.random.fold_in(arg_keys[6], part), 7)
    tokens = scatter_about(part_keys[0], (TOKENS, D), 1.0, 6.0, ((0, 64),))
    expert_ids_keys = jax.random.split(jax.random.fold_in(part_keys[1], 1), TOKENS // TOK_DEV)
    expert_ids_turns = jax.random.permutation(jax.random.fold_in(part_keys[1], 3), TOKENS // TOK_DEV)
    expert_ids = jax.vmap(lambda own, number: shared_out(jax.random.fold_in(part_keys[1], 2), own, number, TOK_DEV, EXPERTS, TOPK, CAP, 1))(expert_ids_keys, expert_ids_turns).reshape((TOKENS, TOPK))
    route_weight = jnp.clip(jnp.exp(math.log(1.0) - 2.9957323 * jax.random.uniform(part_keys[2], (TOKENS, TOPK), jnp.float32) ** steps_of(part_keys[2], (TOKENS, TOPK), ((0, 64),), -0.2, 0.2)), 0.05, 1.0)
    w_gate = scatter_about(arg_keys[3], (EXPERTS, 2, D, HALF), D ** -0.5, 0.125, ((0, 64),))
    w_up = scatter_about(arg_keys[4], (EXPERTS, 2, D, HALF), D ** -0.5, 0.125, ((0, 64),))
    w_down = scatter_about(arg_keys[5], (EXPERTS, 2, HALF, D), HID ** -0.5, 0.21875, ((0, 64),))
    return dict(tokens=tokens, expert_ids=expert_ids, route_weight=route_weight, w_gate=w_gate, w_up=w_up, w_down=w_down)


def reference(tokens, expert_ids, route_weight, w_gate, w_up, w_down):
    gates = (route_weight / jnp.sum(route_weight, axis=1, keepdims=True)).astype(jnp.bfloat16)
    block_ids = expert_ids.reshape(N_EXPERT, TOK_DEV * TOPK)
    onehot = (block_ids[:, :, None] == jnp.arange(EXPERTS, dtype=jnp.int32)[None, None, :]).astype(jnp.int32)
    before = jnp.cumsum(onehot, axis=1) - onehot
    slot = jnp.sum(before * onehot, axis=2)
    source = jnp.arange(N_EXPERT, dtype=jnp.int32)[:, None]
    per_expert = N_EXPERT * CAP
    position = (block_ids * per_expert + source * CAP + slot).reshape(-1).astype(jnp.int32)
    token_index = (jnp.arange(TOKENS * TOPK, dtype=jnp.int32) // TOPK).astype(jnp.int32)
    table_tok = jnp.zeros((EXPERTS * per_expert,), jnp.int32).at[position].set(token_index)
    table_live = jnp.zeros((EXPERTS * per_expert,), jnp.bfloat16).at[position].set(jnp.ones((TOKENS * TOPK,), jnp.bfloat16))
    table_gate = jnp.zeros((EXPERTS * per_expert,), jnp.bfloat16).at[position].set(gates.reshape(-1))
    table_tok = table_tok.reshape(EXPERTS, per_expert)
    table_live = table_live.reshape(EXPERTS, per_expert)
    table_gate = table_gate.reshape(EXPERTS, per_expert)
    gate_pairs = w_gate.reshape(EXPERTS // 2, 2, 2, D, HALF)
    up_pairs = w_up.reshape(EXPERTS // 2, 2, 2, D, HALF)
    down_pairs = w_down.reshape(EXPERTS // 2, 2, 2, HALF, D)

    def one_expert(expert):
        pair = expert // 2
        inner = expert % 2
        rows = tokens[table_tok[expert]] * table_live[expert][:, None]
        weight_g = table_gate[expert].astype(jnp.float32)[:, None]
        partials = []
        for half in range(2):
            wg = gate_pairs[pair, half, inner]
            wu = up_pairs[pair, half, inner]
            wd = down_pairs[pair, half, inner]
            gate_h = jnp.dot(rows, wg, preferred_element_type=jnp.float32)
            up_h = jnp.dot(rows, wu, preferred_element_type=jnp.float32)
            hidden = (jax.nn.silu(gate_h) * up_h).astype(jnp.bfloat16)
            partial_value = (jnp.dot(hidden, wd, preferred_element_type=jnp.float32) * weight_g).astype(jnp.bfloat16)
            partials.append(partial_value)
        return (partials[0].astype(jnp.float32) + partials[1].astype(jnp.float32)).astype(jnp.bfloat16)

    combined = lax.map(one_expert, jnp.arange(EXPERTS, dtype=jnp.int32))
    flat = combined.reshape(EXPERTS * per_expert, D)
    picked = flat[position].reshape(TOKENS, TOPK, D)
    return jnp.sum(picked.astype(jnp.float32), axis=1).astype(jnp.bfloat16)
```

```python
import jax
import jax.numpy as jnp
from jax import lax
from jax.experimental import pallas as pl
from jax.experimental.pallas import tpu as pltpu
from jax.sharding import PartitionSpec as P

NZ, NY, NC = 8, 4, 2
BF, F32 = jnp.bfloat16, jnp.float32


def moved(value, dz=0, dy=0, dc=0):
    pairs = []
    for z in range(NZ):
        for y in range(NY):
            for c in range(NC):
                there = ((z + dz) % NZ) * 8 + ((y + dy) % NY) * 2 + (c + dc) % NC
                pairs.append((z * 8 + y * 2 + c, there))
    return lax.ppermute(value, "expert", pairs)


def shape(rows, width, dtype=BF):
    return jax.ShapeDtypeStruct((rows, width), dtype)


def call(body, outs, place, args):
    vmem = pl.BlockSpec(memory_space=pltpu.VMEM)
    return pl.pallas_call(
        body,
        out_shape=outs,
        in_specs=[pl.BlockSpec(memory_space=pltpu.SMEM)] + [vmem] * len(args),
        out_specs=[vmem] * len(outs),
        compiler_params=pltpu.CompilerParams(vmem_limit_bytes=56 * 2**20),
    )(place, *args)


def load_body(place, tokens, ids, weight, out):
    del place
    toks, width = tokens.shape
    w = weight[...]
    gates = (w / jnp.sum(w, axis=0, keepdims=True)).astype(BF).astype(F32)
    pad = jnp.zeros((8, width - 2 * toks), F32)
    out[0:toks, :] = tokens[...]
    out[toks : toks + 8, :] = jnp.concatenate([ids[...].astype(F32), gates, pad], axis=1).astype(BF)


def group_rows(nb):
    return 72 if nb == 2 else 40


def choices(place, metas):
    z, y = place[0] // 8, (place[0] % 8) // 2
    toks = metas[0].shape[1] // 2
    which = lax.broadcasted_iota(jnp.int32, (8, toks), 0)
    expert = (8 * z + 2 * ((y + which // 2) % NY) + which % 2).astype(F32)
    earlier = lax.broadcasted_iota(jnp.int32, (toks, toks), 0) < lax.broadcasted_iota(
        jnp.int32, (toks, toks), 1
    )
    earlier = jnp.where(earlier, 1.0, 0.0).astype(BF)
    base = jnp.zeros((8, 1), F32)
    found = []
    for meta in metas:
        member = jnp.zeros((8, toks), F32)
        gate = jnp.zeros((8, toks), F32)
        for k in range(8):
            hit = expert == meta[k : k + 1, :toks]
            member = member + jnp.where(hit, 1.0, 0.0)
            gate = gate + jnp.where(hit, meta[k : k + 1, toks:], 0.0)
        rank = jnp.dot(member.astype(BF), earlier, preferred_element_type=F32)
        found.append((jnp.where(member > 0, rank + base, -1.0), gate))
        base = base + jnp.sum(member, axis=1, keepdims=True)
    return found


def slot_of(rows, pure, toks):
    r = lax.broadcasted_iota(jnp.int32, (rows, toks), 0)
    second = ((r >= pure) & (r < 2 * pure)) | (r >= 2 * pure + 4)
    slot = jnp.where(
        r < 2 * pure,
        jnp.where(second, r - pure, r),
        jnp.where(second, r - pure - 4, r - pure),
    )
    return second, slot.astype(F32)


def pack_body(nb, place, *refs):
    blocks, outs, tables = refs[:nb], refs[nb : nb + NY], refs[nb + NY :]
    toks = blocks[0].shape[0] - 8
    rows = group_rows(nb)
    second, slot = slot_of(rows, 16 * nb, toks)
    total = None
    metas = [b[toks : toks + 8, : 2 * toks].astype(F32) for b in blocks]
    for (v, g), block, table in zip(choices(place, metas), blocks, tables):
        table[0:8, :] = v
        table[8:16, :] = g
        picks = []
        for d in range(NY):
            here = jnp.where(second, v[2 * d + 1 : 2 * d + 2, :], v[2 * d : 2 * d + 1, :])
            picks.append(jnp.where(here == slot, 1.0, 0.0))
        pick = jnp.concatenate(picks, axis=0).astype(BF)
        part = jnp.dot(pick, block[0:toks, :], preferred_element_type=F32)
        total = part if total is None else total + part
    for d in range(NY):
        outs[d][...] = total[d * rows : (d + 1) * rows].astype(BF)


def pack(place, blocks):
    nb, toks, width = len(blocks), blocks[0].shape[0] - 8, blocks[0].shape[1]
    outs = [shape(group_rows(nb), width)] * NY + [shape(16, toks, F32)] * nb
    made = call(lambda *r: pack_body(nb, *r), outs, place, blocks)
    return made[:NY], made[NY:]


def combine_body(nb, n_in, last, place, *refs):
    del place
    tables, rows_in = refs[:nb], refs[nb : nb + NY]
    sums, outs = refs[nb + NY : nb + NY + n_in], refs[nb + NY + n_in :]
    rows, toks = group_rows(nb), tables[0].shape[1]
    second, slot = slot_of(rows, 16 * nb, toks)
    got = jnp.concatenate([r[...].astype(F32) for r in rows_in], axis=0).astype(BF)
    for b, table in enumerate(tables):
        v, g = table[0:8, :], table[8:16, :]
        picks = []
        for d in range(NY):
            here = jnp.where(second, v[2 * d + 1 : 2 * d + 2, :], v[2 * d : 2 * d + 1, :])
            gate = jnp.where(second, g[2 * d + 1 : 2 * d + 2, :], g[2 * d : 2 * d + 1, :])
            picks.append(jnp.where(here == slot, gate, 0.0))
        pick = jnp.concatenate(picks, axis=0).astype(BF)
        part = lax.dot_general(pick, got, (((0,), (0,)), ((), ())), preferred_element_type=F32)
        for i in range(n_in):
            if last or i == b:
                part = part + sums[i][...].astype(F32)
        outs[b][...] = part.astype(BF)


def combine(place, tables, rows_in, sums, last=False):
    nb, toks, width = len(tables), tables[0].shape[1], rows_in[0].shape[1]
    return call(
        lambda *r: combine_body(nb, len(sums), last, *r),
        [shape(toks, width)] * nb, place, [*tables, *rows_in, *sums],
    )


def experts_body(pures, *refs):
    n = NY * len(pures)
    xs, weights = refs[:n], refs[n : n + 6]
    outs = refs[n + 6 :]
    pure = [p for p in pures for _ in range(NY)]
    j = pl.program_id(0)
    mixed = jnp.concatenate([x[2 * p : 2 * p + 8, :].astype(F32) for x, p in zip(xs, pure)], axis=0)
    at = [pl.multiple_of(j * p, p) for p in pure]
    x = jnp.concatenate(
        [x[pl.ds(a, p), :] for x, a, p in zip(xs, at, pure)] + [mixed.astype(BF)], axis=0
    )
    total = None
    for h in range(2):
        w_g, w_u, w_d = weights[3 * h : 3 * h + 3]
        gate = jnp.dot(x, w_g[0], preferred_element_type=F32)
        up = jnp.dot(x, w_u[0], preferred_element_type=F32)
        hidden = (gate / (1.0 + jnp.exp(-gate)) * up).astype(BF)
        part = jnp.dot(hidden, w_d[0], preferred_element_type=F32)
        total = part if total is None else total + part
    row = 0
    for out, a, p in zip(outs, at, pure):
        out[pl.ds(a, p), :] = total[row : row + p].astype(BF)
        row += p
    tails = [total[row + 8 * i : row + 8 * i + 8] for i in range(n)]

    @pl.when(j == 0)
    def _():
        for out, p, tail in zip(outs, pure, tails):
            out[2 * p : 2 * p + 8, :] = tail.astype(BF)

    @pl.when(j == 1)
    def _():
        first = lax.broadcasted_iota(jnp.int32, tails[0].shape, 0) < 4
        for out, p, tail in zip(outs, pure, tails):
            old = out[2 * p : 2 * p + 8, :].astype(F32)
            out[2 * p : 2 * p + 8, :] = jnp.where(first, old, tail).astype(BF)


def experts(sizes, groups, weights):
    xs = [x for g in groups for x in g]
    whole = [pl.BlockSpec(x.shape, lambda j: (0, 0)) for x in xs]
    kernel = pl.pallas_call(
        lambda *r: experts_body([16 * nb for nb in sizes], *r),
        grid=(2,),
        out_shape=[shape(*x.shape) for x in xs],
        in_specs=whole + [pl.BlockSpec((1,) + w.shape[1:], lambda j: (j, 0, 0)) for w in weights],
        out_specs=whole,
        compiler_params=pltpu.CompilerParams(vmem_limit_bytes=56 * 2**20),
    )
    made = kernel(*xs, *weights)
    return [made[i : i + NY] for i in range(0, len(made), NY)]


def on_device(tokens, expert_ids, route_weight, w_gate, w_up, w_down):
    toks, width = tokens.shape
    place = lax.axis_index("expert").astype(jnp.int32).reshape(1)
    (own,) = call(
        load_body, [shape(toks + 8, width)], place, [tokens, expert_ids.T, route_weight.T]
    )

    block = {0: own}
    for m in (1, 2, 3, 4):
        block[m] = moved(block[m - 1], dz=-1)
        if m < 4:
            block[-m] = moved(block[1 - m], dz=1)

    mine = (w_gate[0], w_up[0], w_down[0])
    weights = mine + tuple(moved(w, dc=1) for w in mine)

    got, tables = [], []
    for ms in [(0,), (1, -1), (2, -2), (3, -3), (4,)]:
        sent, table = pack(place, [block[m] for m in ms])
        got.append([sent[0]] + [moved(sent[d], dy=d) for d in range(1, NY)])
        tables.append(table)

    early = experts([1, 2, 2], got[:3], weights)
    late = experts([2, 1], got[3:], weights)
    back = [[out[0]] + [moved(out[d], dy=-d) for d in range(1, NY)] for out in early + late]

    (far,) = combine(place, tables[4], back[4], [])
    sums = [moved(far, dz=1)]
    for i in (3, 2, 1):
        outs = combine(place, tables[i], back[i], sums)
        sums = [moved(outs[0], dz=1), moved(outs[1], dz=-1)]
    (mixed,) = combine(place, tables[0], back[0], sums, last=True)
    return mixed


def solution(mesh):
    return jax.shard_map(
        on_device,
        mesh=mesh,
        in_specs=(
            P(("dp", "expert"), None),
            P(("dp", "expert"), None),
            P(("dp", "expert"), None),
            P("expert", None, None, None),
            P("expert", None, None, None),
            P("expert", None, None, None),
        ),
        out_specs=P(("dp", "expert"), None),
        check_vma=False,
    )
```
